128 devices in a mesh: pipe: 4 (over x), seq: 8 (over z, y_hi), mp: 4 (over y_lo, core).
Axes of the slice: x: 4, y: 4 (y_hi: 2, y_lo: 2; y = y_hi * 2 + y_lo), z: 4, core: 2. Of those that a mesh axis runs over, the one named last changes fastest.
Arguments:
- enc_in: bfloat16 [2, 512, 4096], P(None, 'seq'), may hold values from -6 to 6
- dec_in: bfloat16 [2, 512, 4096], P(None, 'seq'), may hold values from -6 to 6
- doc_ids: int32 [2, 512], replicated, may hold values from 0 to 1, as said below
- enc_sections: int32 [1], replicated, may hold values from 1 to 3
- norm_gain: float32 [4, 4096], P('pipe'), may hold values from 0.1 to 1.9
- q_weight: bfloat16 [4, 4096, 2048], P('pipe', None, 'mp'), may hold values from -0.09375 to 0.09375
- k_weight: bfloat16 [4, 4096, 2048], P('pipe', None, 'mp'), may hold values from -0.09375 to 0.09375
- v_weight: bfloat16 [4, 4096, 2048], P('pipe', None, 'mp'), may hold values from -0.09375 to 0.09375
- o_weight: bfloat16 [4, 2048, 4096], P('pipe', 'mp'), may hold values from -1.25 to 1.25
- out_grad: bfloat16 [2, 512, 4096], P(None, 'seq'), may hold values from -6 to 6
Outputs:
- section_out: bfloat16 [4, 2, 512, 4096], P('pipe', None, 'seq', 'mp')
- section_grad: bfloat16 [4, 2, 2, 512, 4096], P('pipe', None, None, 'seq', 'mp')
The draws below stay inside these ranges and needn't reach their ends.
Inputs may be any that keep to these rules, and one draw needn't show every extreme that they name: `doc_ids`: ids of the two documents that each micro-batch's window holds, shared by its encoder and decoder positions; 0 up to a boundary, 1 after it, each document 64 // 2 or more positions long. Sections with an index below enc_sections[0] are encoder sections, the others decoder sections.
All inputs are finite; a program needn't handle non-finite values.
Results may differ from the reference program's by a relative error of at most 0.034.
Values may be sent and summed in bfloat16 or wider, within the bound.
No kernel may reach another device: no remote copies, remote signals or barrier semaphores. Data moves between devices by JAX's collectives and lax.ppermute only.
A program may use at most 192 MiB of HBM per device.

```python
import jax
import jax.numpy as jnp
from jax import lax

D = 4096
HEADS = 8
HS = 256
MB = 2
TOK_DEV = 64
L = 512
N_PIPE = 4


def draw_doc_ids(key, part):
    boundary = jax.random.randint(key, (MB, 1), TOK_DEV // 2, L - TOK_DEV // 2 + 1)
    positions = jnp.arange(L, dtype=jnp.int32)[None, :]
    return (positions >= boundary).astype(jnp.int32)


def shard_levels(key, extent, pieces, low, largest):
    level = 1.0
    for axis_at, blocks in pieces:
        draws = jax.random.uniform(jax.random.fold_in(jax.random.fold_in(key, 6), axis_at), (blocks,), jnp.float32, low / len(pieces), largest / len(pieces))
        level = level * jnp.repeat(jnp.exp(draws), extent[axis_at] // blocks).reshape((-1,) + (1,) * (len(extent) - 1 - axis_at))
    return level


def bell_draw(stream_key, shape, width, bound, pieces=(), kind=jnp.bfloat16):
    result = jax.random.normal(stream_key, shape, jnp.float32) * width
    if len(pieces) > 0:
        result = shard_levels(stream_key, shape, pieces, -0.22, 0.18) * result
    return jnp.clip(result, min=-bound, max=bound).astype(kind)


def setup_inputs(seed: int = 0) -> dict:
    splits = jax.random.split(jax.random.key(seed), 11)
    enc_in = bell_draw(splits[0], (MB, L, D), 1.0, 6.0, ((1, 8),))
    dec_in = bell_draw(splits[1], (MB, L, D), 1.0, 6.0, ((1, 8),))
    doc_ids = draw_doc_ids(jax.random.fold_in(splits[10], 71), 0)
    enc_sections = jax.random.randint(splits[3], (1,), 1, N_PIPE).astype(jnp.int32)
    norm_gain = jnp.clip(1.0 + 0.18 * jax.random.normal(splits[4], (N_PIPE, D), jnp.float32), 0.1, 1.9)
    q_weight = bell_draw(splits[5], (N_PIPE, D, HEADS * HS), D ** -0.5, 0.09375, ((0, 4), (2, 4)))
    k_weight = bell_draw(splits[6], (N_PIPE, D, HEADS * HS), D ** -0.5, 0.09375, ((0, 4), (2, 4)))
    v_weight = bell_draw(splits[7], (N_PIPE, D, HEADS * HS), D ** -0.5, 0.09375, ((0, 4), (2, 4)))
    o_weight = bell_draw(splits[8], (N_PIPE, HEADS * HS, D), (4.0 * (HEADS * HS) ** -0.5), 1.25, ((0, 4), (1, 4)))
    out_grad = bell_draw(splits[9], (MB, L, D), 1.0, 6.0, ((1, 8),))
    return {"enc_in": enc_in, "dec_in": dec_in, "doc_ids": doc_ids, "enc_sections": enc_sections, "norm_gain": norm_gain, "q_weight": q_weight, "k_weight": k_weight, "v_weight": v_weight, "o_weight": o_weight, "out_grad": out_grad}


epsilon = 1e-06

def widened(values):
    return lax.optimization_barrier(values).astype(jnp.float32)

def row_norm(stream, stream_gain):
    values = stream.astype(jnp.float32)
    factor = lax.rsqrt(lax.optimization_barrier(jnp.mean(values * values, axis=-1, keepdims=True)) + epsilon)
    return ((values * factor * stream_gain).astype(jnp.bfloat16), factor)

def head_norm(projected, head_count):
    shaped = projected.reshape(projected.shape[0], head_count, -1)
    factor = lax.rsqrt(lax.optimization_barrier(jnp.mean(shaped * shaped, axis=-1, keepdims=True)) + epsilon)
    return ((shaped * factor).astype(jnp.bfloat16), factor)

def norm_back(stream, factor, stream_gain, incoming):
    values = stream.astype(jnp.float32)
    scaled = stream_gain * incoming
    return factor * (scaled - values * factor * factor * lax.optimization_barrier(jnp.mean(scaled * values, axis=-1, keepdims=True)))

def head_back(normed, factor, incoming):
    values = normed.astype(jnp.float32)
    return factor * (incoming - values * lax.optimization_barrier(jnp.mean(incoming * values, axis=-1, keepdims=True)))

def attend_keys(queries, keys, same_doc):
    scores = jnp.einsum('thd,khd->htk', widened(queries), widened(keys)) * HS ** (-0.5)
    weights = jnp.where(same_doc[None], jnp.exp(scores), jnp.float32(0.0))
    return (weights, lax.optimization_barrier(jnp.sum(weights, axis=-1)))

def section_forward(enc_stream, dec_stream, encoder, stream_gain, query_map, key_map, value_map, out_map, doc_row):
    source = jnp.where(encoder, enc_stream, dec_stream)
    q_in, q_factor = row_norm(source, stream_gain)
    m_in, m_factor = row_norm(enc_stream, stream_gain)
    queries, q_head = head_norm(jnp.dot(q_in, query_map, preferred_element_type=jnp.float32), HEADS)
    keys, k_head = head_norm(jnp.dot(m_in, key_map, preferred_element_type=jnp.float32), HEADS)
    values = jnp.dot(m_in, value_map, preferred_element_type=jnp.float32).astype(jnp.bfloat16)
    values = values.reshape(values.shape[0], HEADS, HS)
    same_doc = doc_row[:, None] == doc_row[None, :]
    weights, totals = attend_keys(queries, keys, same_doc)
    summed = jnp.einsum('htk,khd->thd', widened(weights.astype(jnp.bfloat16)), widened(values))
    attended = (summed / jnp.transpose(totals)[:, :, None]).astype(jnp.bfloat16)
    branch = jnp.dot(attended.reshape(attended.shape[0], -1), out_map, preferred_element_type=jnp.float32)
    updated = (source.astype(jnp.float32) + branch).astype(jnp.bfloat16)
    kept = (source, q_factor, m_factor, queries, q_head, keys, k_head, values, same_doc, attended)
    return (updated, kept)

def section_backward(enc_stream, grad_enc, grad_dec, encoder, stream_gain, query_map, key_map, value_map, out_map, kept):
    source, q_factor, m_factor, queries, q_head, keys, k_head, values, same_doc, attended = kept
    row_count = source.shape[0]
    score_scale = HS ** (-0.5)
    upstream = jnp.where(encoder, grad_enc, grad_dec)
    d_attended = jnp.dot(upstream, out_map.T, preferred_element_type=jnp.float32).astype(jnp.bfloat16)
    d_attended = d_attended.reshape(row_count, HEADS, HS)
    weights, totals = attend_keys(queries, keys, same_doc)
    portion = weights / totals[:, :, None]
    portion_low = portion.astype(jnp.bfloat16)
    along_values = jnp.einsum('thd,khd->htk', widened(d_attended), widened(values))
    delta_rows = lax.optimization_barrier(jnp.sum(widened(d_attended) * widened(attended), axis=-1))
    d_scores = (portion * (along_values - jnp.transpose(delta_rows)[:, :, None])).astype(jnp.bfloat16)
    d_queries = jnp.einsum('htk,khd->thd', widened(d_scores), widened(keys)) * score_scale
    d_keys = jnp.einsum('htk,thd->khd', widened(d_scores), widened(queries)) * score_scale
    d_values = jnp.einsum('htk,thd->khd', widened(portion_low), widened(d_attended)).astype(jnp.bfloat16)
    q_grad = head_back(queries, q_head, d_queries).astype(jnp.bfloat16).reshape(row_count, -1)
    k_grad = head_back(keys, k_head, d_keys).astype(jnp.bfloat16).reshape(row_count, -1)
    d_q_in = jnp.dot(q_grad, query_map.T, preferred_element_type=jnp.float32)
    d_m_in = jnp.dot(k_grad, key_map.T, preferred_element_type=jnp.float32)
    d_m_in = d_m_in + jnp.dot(d_values.reshape(row_count, -1), value_map.T, preferred_element_type=jnp.float32)
    back_q = norm_back(source, q_factor, stream_gain, d_q_in)
    back_m = norm_back(enc_stream, m_factor, stream_gain, d_m_in)
    new_enc = (grad_enc.astype(jnp.float32) + back_m + jnp.where(encoder, back_q, 0.0)).astype(jnp.bfloat16)
    new_dec = (grad_dec.astype(jnp.float32) + jnp.where(encoder, 0.0, back_q)).astype(jnp.bfloat16)
    return (new_enc, new_dec)

def reference(enc_in, dec_in, doc_ids, enc_sections, norm_gain, q_weight, k_weight, v_weight, o_weight, out_grad):
    outs_all = [[None] * MB for section_id in range(N_PIPE)]
    grads_enc = [[None] * MB for section_id in range(N_PIPE)]
    grads_dec = [[None] * MB for section_id in range(N_PIPE)]
    for batch_id in range(MB):
        enc_stream = enc_in[batch_id]
        dec_stream = dec_in[batch_id]
        doc_row = doc_ids[batch_id]
        inputs_kept = []
        for section_id in range(N_PIPE):
            encoder = section_id < enc_sections[0]
            updated, kept = section_forward(enc_stream, dec_stream, encoder, norm_gain[section_id], q_weight[section_id], k_weight[section_id], v_weight[section_id], o_weight[section_id], doc_row)
            inputs_kept.append((enc_stream, kept))
            outs_all[section_id][batch_id] = updated
            enc_stream = jnp.where(encoder, updated, enc_stream)
            dec_stream = jnp.where(encoder, dec_stream, updated)
        grad_enc = jnp.zeros_like(out_grad[batch_id])
        grad_dec = out_grad[batch_id]
        for section_id in range(N_PIPE - 1, -1, -1):
            encoder = section_id < enc_sections[0]
            enc_before, kept = inputs_kept[section_id]
            grad_enc, grad_dec = section_backward(enc_before, grad_enc, grad_dec, encoder, norm_gain[section_id], q_weight[section_id], k_weight[section_id], v_weight[section_id], o_weight[section_id], kept)
            grads_enc[section_id][batch_id] = grad_enc
            grads_dec[section_id][batch_id] = grad_dec
    section_out = jnp.stack([jnp.stack(rows_list) for rows_list in outs_all])
    section_grad = jnp.stack([jnp.stack([jnp.stack(grads_enc[section_id]), jnp.stack(grads_dec[section_id])]) for section_id in range(N_PIPE)])
    return (section_out, section_grad)
```

```python
import jax
import jax.numpy as jnp
from jax import lax
from jax.sharding import PartitionSpec as P

HEADS = 8
HS = 256
epsilon = 1e-06
N_PIPE = 4
N_Z = 4
BF = jnp.bfloat16
F32 = jnp.float32


def mp_send(x, moves):
    pairs = []
    for src, dst, flip_y, flip_c in moves:
        for y_lo in range(2):
            for core in range(2):
                pairs.append(
                    (src * 4 + y_lo * 2 + core, dst * 4 + (y_lo ^ flip_y) * 2 + (core ^ flip_c))
                )
    return lax.ppermute(x, ("pipe", "mp"), pairs)


def core_swap(x, pipes):
    return mp_send(x, [(p, p, 0, 1) for p in pipes])


def chip_swap(x, pipes):
    return mp_send(x, [(p, p, 1, 0) for p in pipes])


def z_send(x, by, pipes):
    pairs = []
    for p in pipes:
        for z in range(N_Z):
            for y_hi in range(2):
                pairs.append((p * 8 + z * 2 + y_hi, p * 8 + ((z + by) % N_Z) * 2 + y_hi))
    return lax.ppermute(x, ("pipe", "seq"), pairs)


def half_swap(x, pipes):
    pairs = []
    for p in pipes:
        for z in range(N_Z):
            for y_hi in range(2):
                pairs.append((p * 8 + z * 2 + y_hi, p * 8 + z * 2 + 1 - y_hi))
    return lax.ppermute(x, ("pipe", "seq"), pairs)


def per_device(
    enc_in,
    dec_in,
    doc_ids,
    enc_sections,
    norm_gain,
    q_weight,
    k_weight,
    v_weight,
    o_weight,
    out_grad,
):
    pipe = lax.axis_index("pipe")
    mp = lax.axis_index("mp")
    seq = lax.axis_index("seq")
    y_lo = mp // 2
    core = mp % 2
    z = seq // 2
    y_hi = seq % 2
    tok = enc_in.shape[1]
    width = enc_in.shape[2]
    rows = 2 * tok
    share = width // 4
    heads = HEADS // 4
    head_width = heads * HS
    scale = HS ** (-0.5)
    gain = norm_gain[0]
    query_map = q_weight[0]
    key_map = k_weight[0]
    value_map = v_weight[0]
    out_map = o_weight[0]

    def cut(x):
        return lax.dynamic_slice_in_dim(x, mp * share, share, x.ndim - 1)

    gain_own = cut(gain)

    def pick_half(x, which):
        return lax.dynamic_index_in_dim(x, which, 0, keepdims=False)

    doc_row = pick_half(doc_ids, y_hi)

    def block_docs(z_from):
        first = lax.dynamic_slice_in_dim(doc_row, (z_from * 2 + y_hi) * tok, tok)
        second = lax.dynamic_slice_in_dim(doc_row, (z_from * 2 + 1 - y_hi) * tok, tok)
        return jnp.concatenate([first, second])

    key_docs = jnp.concatenate([block_docs((z - r) % N_Z) for r in range(N_Z)])
    same_doc = key_docs[:rows, None] == key_docs[None, :]

    def order_columns(a, b, ra, rb):
        low_y = y_lo == 0
        low_c = core == 0
        m0, m1 = jnp.where(low_y, a, b), jnp.where(low_y, b, a)
        s0, s1 = jnp.where(low_y, ra, rb), jnp.where(low_y, rb, ra)
        return jnp.concatenate(
            [
                jnp.where(low_c, m0, s0),
                jnp.where(low_c, s0, m0),
                jnp.where(low_c, m1, s1),
                jnp.where(low_c, s1, m1),
            ],
            1,
        )

    def gather_columns(a, pipes):
        b = chip_swap(a, pipes)
        ra = core_swap(a, pipes)
        rb = core_swap(b, pipes)
        return order_columns(a, b, ra, rb)

    def shift_columns(x, src, dst):
        a = mp_send(x, [(src, dst, 0, 0)])
        b = mp_send(x, [(src, dst, 1, 0)])
        ra = core_swap(a, [dst])
        rb = core_swap(b, [dst])
        return order_columns(a, b, ra, rb)

    def reduce_columns(partial, pipes):
        low = partial.astype(BF).reshape(rows, 2, 2, share)
        keep = pick_half(jnp.transpose(low, (2, 0, 1, 3)), core)
        away = pick_half(jnp.transpose(low, (2, 0, 1, 3)), 1 - core)
        got = core_swap(away, pipes)
        both = keep.astype(F32) + got.astype(F32)
        mine = lax.dynamic_index_in_dim(both, y_lo, 1, keepdims=False)
        away = lax.dynamic_index_in_dim(both, 1 - y_lo, 1, keepdims=False).astype(BF)
        return mine + chip_swap(away, pipes).astype(F32)

    def reduce_stat(stat, pipes):
        stat = stat + core_swap(stat, pipes)
        return stat + chip_swap(stat, pipes)

    def row_norm(x):
        values = x.astype(F32)
        factor = lax.rsqrt(jnp.mean(values * values, axis=-1, keepdims=True) + epsilon)
        return (values * factor * gain).astype(BF), factor

    def head_norm(projected):
        shaped = projected.reshape(rows, heads, HS)
        factor = lax.rsqrt(jnp.mean(shaped * shaped, axis=-1, keepdims=True) + epsilon)
        return (shaped * factor).astype(BF), factor

    def head_back(normed, factor, incoming):
        values = normed.astype(F32)
        return factor * (incoming - values * jnp.mean(incoming * values, axis=-1, keepdims=True))

    def project(x, weight):
        return jnp.dot(x, weight, preferred_element_type=F32)

    def project_back(x, weight):
        return jnp.einsum("tc,dc->td", x, weight, preferred_element_type=F32)

    def make_keys(m_in, pipes):
        keys, k_head = head_norm(project(m_in, key_map))
        values = project(m_in, value_map).astype(BF).reshape(rows, heads, HS)
        key_all = jnp.concatenate([keys] + [z_send(keys, r, pipes) for r in (1, 2, 3)], 0)
        value_all = jnp.concatenate([values] + [z_send(values, r, pipes) for r in (1, 2, 3)], 0)
        return keys, k_head, values, key_all, value_all

    def attend(queries, key_all, value_all):
        scores = jnp.einsum("thd,khd->htk", queries, key_all, preferred_element_type=F32) * scale
        weights = jnp.where(same_doc[None], jnp.exp(scores), 0.0)
        totals = jnp.sum(weights, axis=-1)
        summed = jnp.einsum(
            "htk,khd->thd", weights.astype(BF), value_all, preferred_element_type=F32
        )
        attended = (summed / jnp.transpose(totals)[:, :, None]).astype(BF)
        portion = weights / totals[:, :, None]
        return attended, portion

    def query_back(grad, queries, q_head, key_all, value_all, attended, portion):
        d_att = project_back(grad, out_map).astype(BF).reshape(rows, heads, HS)
        along = jnp.einsum("thd,khd->htk", d_att, value_all, preferred_element_type=F32)
        delta = jnp.sum(d_att.astype(F32) * attended.astype(F32), axis=-1)
        d_scores = (portion * (along - jnp.transpose(delta)[:, :, None])).astype(BF)
        d_queries = (
            jnp.einsum("htk,khd->thd", d_scores, key_all, preferred_element_type=F32) * scale
        )
        q_grad = head_back(queries, q_head, d_queries).astype(BF)
        stat = jnp.sum(q_grad.astype(F32) * queries.astype(F32) / q_head, axis=(1, 2))
        return d_att, d_scores, q_grad.reshape(rows, -1), stat

    def key_back(d_att, d_scores, portion_low, queries, keys, k_head, values, pipes):
        d_vals = jnp.einsum("htk,thd->khd", portion_low, d_att, preferred_element_type=F32)
        d_keys = jnp.einsum("htk,thd->khd", d_scores, queries, preferred_element_type=F32) * scale
        both = jnp.concatenate(
            [d_vals.reshape(N_Z * rows, -1), d_keys.reshape(N_Z * rows, -1)], 1
        )
        total = both[:rows]
        for r in (1, 2, 3):
            total = total + z_send(
                both[r * rows : (r + 1) * rows].astype(BF), N_Z - r, pipes
            ).astype(F32)
        d_values = total[:, :head_width].astype(BF)
        k_grad = head_back(keys, k_head, total[:, head_width:].reshape(rows, heads, HS)).astype(BF)
        stat = jnp.sum(k_grad.astype(F32) * keys.astype(F32) / k_head, axis=(1, 2))
        stat = stat + jnp.sum(
            d_values.astype(F32) * values.reshape(rows, -1).astype(F32), axis=1
        )
        return d_values, k_grad.reshape(rows, -1), stat

    def norm_back(own, factor, d_own, stat):
        mean = (stat / width)[:, None] / factor
        return factor * (gain_own * d_own - own.astype(F32) * factor * factor * mean)

    def by_pipe(choices):
        items = list(choices.items())
        out = items[-1][1]
        for p, value in items[:-1]:
            out = jnp.where(pipe == p, value, out)
        return out

    def run(enc_count):
        dec_pipes = list(range(enc_count, N_PIPE))

        def swap_direct(x, p):
            keep = pick_half(x, y_hi)
            got = half_swap(pick_half(x, 1 - y_hi), [p])
            return jnp.concatenate([keep, got], 0)

        first = jnp.concatenate(
            [
                cut(pick_half(enc_in, y_hi)),
                half_swap(cut(pick_half(enc_in, 1 - y_hi)), [0]),
            ],
            0,
        )
        enc_full = gather_columns(first, [0])
        dec_full = swap_direct(dec_in, enc_count)
        top_grad = swap_direct(out_grad, N_PIPE - 1)
        top_grad = jnp.where(pipe == N_PIPE - 1, top_grad, jnp.zeros_like(top_grad))
        outs = {}
        saved = {}
        for s in range(enc_count):
            m_in, factor = row_norm(enc_full)
            own = cut(enc_full)
            keys, k_head, values, key_all, value_all = make_keys(m_in, [s])
            queries, q_head = head_norm(project(m_in, query_map))
            attended, portion = attend(queries, key_all, value_all)
            saved[s] = (
                own, factor, queries, q_head, keys, k_head, values, key_all, value_all,
                attended, portion,
            )
            branch = reduce_columns(project(attended.reshape(rows, -1), out_map), [s])
            updated = (own.astype(F32) + branch).astype(BF)
            outs[s] = updated
            if s + 1 < enc_count:
                enc_full = shift_columns(updated, s, s + 1)
        last = enc_count - 1
        sent = [mp_send(outs[last], [(last, p, 0, 0)]) for p in dec_pipes]
        enc_piece = by_pipe(dict(zip(dec_pipes, sent)))
        enc_full = gather_columns(enc_piece, dec_pipes)
        m_in, m_factor = row_norm(enc_full)
        keys, k_head, values, key_all, value_all = make_keys(m_in, dec_pipes)
        for s in dec_pipes:
            q_in, factor = row_norm(dec_full)
            own = cut(dec_full)
            queries, q_head = head_norm(project(q_in, query_map))
            attended, portion = attend(queries, key_all, value_all)
            saved[s] = (own, factor, queries, q_head, attended, portion)
            branch = reduce_columns(project(attended.reshape(rows, -1), out_map), [s])
            updated = (own.astype(F32) + branch).astype(BF)
            outs[s] = updated
            if s + 1 < N_PIPE:
                dec_full = shift_columns(updated, s, s + 1)
        grad = top_grad
        dec_grads = {}
        enc_grads = {}
        d_att_sum = None
        for s in reversed(dec_pipes):
            own, factor, queries, q_head, attended, portion = saved[s]
            d_att, d_scores, q_grad, stat = query_back(
                grad, queries, q_head, key_all, value_all, attended, portion
            )
            if d_att_sum is None:
                d_att_sum, d_scores_sum = d_att, d_scores
            else:
                d_att_sum, d_scores_sum = d_att_sum + d_att, d_scores_sum + d_scores
            stat = reduce_stat(stat, [s])
            d_own = reduce_columns(project_back(q_grad, query_map), [s])
            back_q = norm_back(own, factor, d_own, stat)
            new_grad = (cut(grad).astype(F32) + back_q).astype(BF)
            dec_grads[s] = new_grad
            if s > enc_count:
                grad = shift_columns(new_grad, s, s - 1)
        portion_low = by_pipe({s: saved[s][5].astype(BF) for s in dec_pipes})
        queries = by_pipe({s: saved[s][2] for s in dec_pipes})
        d_values, k_grad, stat = key_back(
            d_att_sum, d_scores_sum, portion_low, queries, keys, k_head, values, dec_pipes
        )
        stat = reduce_stat(stat, dec_pipes)
        d_own = reduce_columns(
            project_back(k_grad, key_map) + project_back(d_values, value_map), dec_pipes
        )
        back_m = norm_back(enc_piece, m_factor, d_own, stat)
        back_low = back_m.astype(BF)
        total = jnp.where(pipe >= enc_count, back_m, jnp.zeros_like(back_m))
        for by in range(1, N_PIPE - enc_count + 1):
            moves = [
                (p, p - by, 0, 0) for p in dec_pipes if p - by >= enc_count - 1
            ]
            total = total + mp_send(back_low, moves).astype(F32)
        total = total.astype(BF)
        for s in dec_pipes:
            enc_grads[s] = total
        grad_own = total
        grad = gather_columns(total, [last])
        passed = [mp_send(dec_grads[enc_count], [(enc_count, p, 0, 0)]) for p in range(enc_count)]
        for p in range(enc_count):
            dec_grads[p] = passed[p]
        for s in reversed(range(enc_count)):
            (
                own, factor, queries, q_head, keys, k_head, values, key_all, value_all,
                attended, portion,
            ) = saved[s]
            d_att, d_scores, q_grad, stat = query_back(
                grad, queries, q_head, key_all, value_all, attended, portion
            )
            d_values, k_grad, k_stat = key_back(
                d_att, d_scores, portion.astype(BF), queries, keys, k_head, values, [s]
            )
            stat = reduce_stat(stat + k_stat, [s])
            partial = (
                project_back(q_grad, query_map)
                + project_back(k_grad, key_map)
                + project_back(d_values, value_map)
            )
            d_own = reduce_columns(partial, [s])
            back = norm_back(own, factor, d_own, stat)
            new_grad = (cut(grad).astype(F32) + back).astype(BF)
            enc_grads[s] = new_grad
            if s > 0:
                grad = shift_columns(new_grad, s, s - 1)
        everyone = list(range(N_PIPE))

        def finish(choices):
            own = by_pipe(choices)
            keep = own[:tok]
            got = half_swap(own[tok:], everyone)
            return jnp.stack([jnp.where(y_hi == 0, keep, got), jnp.where(y_hi == 0, got, keep)])

        section_out = finish(outs)[None]
        section_grad = jnp.stack([finish(enc_grads), finish(dec_grads)])[None]
        return section_out, section_grad

    which = jnp.clip(enc_sections[0] - 1, 0, N_PIPE - 2)
    return lax.switch(which, [lambda n=n: run(n) for n in range(1, N_PIPE)])


def solution(mesh):
    return jax.shard_map(
        per_device,
        mesh=mesh,
        in_specs=(
            P(None, "seq", None),
            P(None, "seq", None),
            P(),
            P(),
            P("pipe", None),
            P("pipe", None, "mp"),
            P("pipe", None, "mp"),
            P("pipe", None, "mp"),
            P("pipe", "mp", None),
            P(None, "seq", None),
        ),
        out_specs=(P("pipe", None, "seq", "mp"), P("pipe", None, None, "seq", "mp")),
        check_vma=False,
    )
```

```python
import jax
import jax.numpy as jnp
from jax import lax
from jax.sharding import PartitionSpec as P

HEADS = 8
HS = 256
epsilon = 1e-06
N_PIPE = 4
N_Z = 4
BF = jnp.bfloat16
F32 = jnp.float32


def pipe_send(x, by, flip_y=0):
    pairs = []
    for p in range(N_PIPE):
        for place in range(4):
            pairs.append((p * 4 + place, ((p + by) % N_PIPE) * 4 + (place ^ (2 * flip_y))))
    return lax.ppermute(x, ("pipe", "mp"), pairs)


def core_swap(x):
    return lax.ppermute(x, "mp", [(i, i ^ 1) for i in range(4)])


def chip_swap(x):
    return lax.ppermute(x, "mp", [(i, i ^ 2) for i in range(4)])


def z_send(x, by):
    return lax.ppermute(x, "seq", [(i, (i + 2 * by) % (2 * N_Z)) for i in range(2 * N_Z)])


def half_swap(x):
    return lax.ppermute(x, "seq", [(i, i ^ 1) for i in range(2 * N_Z)])


def per_device(
    enc_in,
    dec_in,
    doc_ids,
    enc_sections,
    norm_gain,
    q_weight,
    k_weight,
    v_weight,
    o_weight,
    out_grad,
):
    pipe = lax.axis_index("pipe")
    mp = lax.axis_index("mp")
    seq = lax.axis_index("seq")
    y_lo = mp // 2
    core = mp % 2
    z = seq // 2
    y_hi = seq % 2
    tok = enc_in.shape[1]
    width = enc_in.shape[2]
    rows = 2 * tok
    share = width // 4
    heads = HEADS // 4
    head_width = heads * HS
    scale = HS ** (-0.5)
    gain = norm_gain[0]
    query_map = q_weight[0]
    key_map = k_weight[0]
    value_map = v_weight[0]
    out_map = o_weight[0]

    def cut(x):
        return lax.dynamic_slice_in_dim(x, mp * share, share, x.ndim - 1)

    gain_own = cut(gain)

    def pick_half(x, which):
        return lax.dynamic_index_in_dim(x, which, 0, keepdims=False)

    doc_row = pick_half(doc_ids, y_hi)

    def block_docs(z_from):
        first = lax.dynamic_slice_in_dim(doc_row, (z_from * 2 + y_hi) * tok, tok)
        second = lax.dynamic_slice_in_dim(doc_row, (z_from * 2 + 1 - y_hi) * tok, tok)
        return jnp.concatenate([first, second])

    key_docs = jnp.concatenate([block_docs((z - r) % N_Z) for r in range(N_Z)])
    same_doc = key_docs[:rows, None] == key_docs[None, :]

    def order_columns(a, b, ra, rb):
        low_y = y_lo == 0
        low_c = core == 0
        m0, m1 = jnp.where(low_y, a, b), jnp.where(low_y, b, a)
        s0, s1 = jnp.where(low_y, ra, rb), jnp.where(low_y, rb, ra)
        return jnp.concatenate(
            [
                jnp.where(low_c, m0, s0),
                jnp.where(low_c, s0, m0),
                jnp.where(low_c, m1, s1),
                jnp.where(low_c, s1, m1),
            ],
            1,
        )

    def gather_columns(a):
        b = chip_swap(a)
        ra = core_swap(a)
        rb = core_swap(b)
        return order_columns(a, b, ra, rb)

    def shift_columns(x, by):
        a = pipe_send(x, by)
        b = pipe_send(x, by, 1)
        ra = core_swap(a)
        rb = core_swap(b)
        return order_columns(a, b, ra, rb)

    def reduce_columns(partial):
        low = partial.astype(BF)
        first = jnp.concatenate([low[:, :share], low[:, 2 * share : 3 * share]], 1)
        second = jnp.concatenate([low[:, share : 2 * share], low[:, 3 * share :]], 1)
        keep = jnp.where(core == 0, first, second)
        away = jnp.where(core == 0, second, first)
        both = keep.astype(F32) + core_swap(away).astype(F32)
        mine = jnp.where(y_lo == 0, both[:, :share], both[:, share:])
        away = jnp.where(y_lo == 0, both[:, share:], both[:, :share]).astype(BF)
        return mine + chip_swap(away).astype(F32)

    def reduce_stat(stat):
        stat = stat + core_swap(stat)
        return stat + chip_swap(stat)

    def row_norm(x):
        values = x.astype(F32)
        factor = lax.rsqrt(jnp.mean(values * values, axis=-1, keepdims=True) + epsilon)
        return (values * factor * gain).astype(BF), factor

    def head(x, h):
        return x[:, h * HS : (h + 1) * HS]

    def head_norm(projected):
        normed, factors = [], []
        for h in range(heads):
            part = head(projected, h)
            factor = lax.rsqrt(jnp.mean(part * part, axis=-1, keepdims=True) + epsilon)
            normed.append((part * factor).astype(BF))
            factors.append(factor)
        return normed, factors

    def head_back(normed, factor, incoming):
        values = normed.astype(F32)
        return factor * (incoming - values * jnp.mean(incoming * values, axis=-1, keepdims=True))

    def project(x, weight):
        return jnp.dot(x, weight, preferred_element_type=F32)

    def times_t(x, y):
        return lax.dot_general(x, y, (((1,), (1,)), ((), ())), preferred_element_type=F32)

    def t_times(x, y):
        return lax.dot_general(x, y, (((0,), (0,)), ((), ())), preferred_element_type=F32)

    def make_keys(m_in):
        keys, k_head = head_norm(project(m_in, key_map))
        values = project(m_in, value_map).astype(BF)
        pair = jnp.concatenate(keys + [values], 1)
        blocks = {r: z_send(pair, r) for r in (2, 1, 3)}
        pair_all = jnp.concatenate([pair, blocks[1], blocks[2], blocks[3]], 0)
        return keys, k_head, values, pair_all

    def weigh(queries, pair_all):
        out = []
        for h in range(heads):
            scores = times_t(queries[h], head(pair_all, h)) * scale
            weights = jnp.where(same_doc, jnp.exp(scores), 0.0)
            out.append((weights, jnp.sum(weights, axis=-1, keepdims=True)))
        return out

    def attend(queries, pair_all):
        attended = []
        weighed = weigh(queries, pair_all)
        for h, (weights, totals) in enumerate(weighed):
            summed = project(weights.astype(BF), head(pair_all, heads + h))
            attended.append((summed / totals).astype(BF))
        return attended

    def query_back(grad, queries, q_head, pair_all, attended):
        d_att = times_t(grad, out_map).astype(BF)
        d_scores, q_grad, portion_low, stat = [], [], [], 0.0
        for h, (weights, totals) in enumerate(weigh(queries, pair_all)):
            portion = weights / totals
            d_h = head(d_att, h)
            along = times_t(d_h, head(pair_all, heads + h))
            delta = jnp.sum(
                d_h.astype(F32) * attended[h].astype(F32), axis=-1, keepdims=True
            )
            d_s = (portion * (along - delta)).astype(BF)
            d_q = project(d_s, head(pair_all, h)) * scale
            grad_h = head_back(queries[h], q_head[h], d_q).astype(BF)
            stat = stat + jnp.sum(
                grad_h.astype(F32) * queries[h].astype(F32), axis=-1
            ) / q_head[h][:, 0]
            d_scores.append(d_s)
            q_grad.append(grad_h)
            portion_low.append(portion.astype(BF))
        return d_att, d_scores, portion_low, jnp.concatenate(q_grad, 1), stat

    def key_back(d_att, d_scores, portion_low, queries, keys, k_head, values):
        both = jnp.concatenate(
            [t_times(d_scores[h], queries[h]) * scale for h in range(heads)]
            + [t_times(portion_low[h], head(d_att, h)) for h in range(heads)],
            1,
        )
        low = both.astype(BF)
        got = {r: z_send(low[r * rows : (r + 1) * rows], N_Z - r) for r in (2, 1, 3)}
        total = both[:rows] + sum(got[r].astype(F32) for r in (1, 2, 3))
        d_values = total[:, head_width:].astype(BF)
        k_grad, stat = [], jnp.sum(d_values.astype(F32) * values.astype(F32), axis=-1)
        for h in range(heads):
            grad_h = head_back(keys[h], k_head[h], head(total, h)).astype(BF)
            stat = stat + jnp.sum(
                grad_h.astype(F32) * keys[h].astype(F32), axis=-1
            ) / k_head[h][:, 0]
            k_grad.append(grad_h)
        return d_values, jnp.concatenate(k_grad, 1), stat

    def norm_back(own, factor, d_own, stat):
        mean = (stat / width)[:, None] / factor
        return factor * (gain_own * d_own - own.astype(F32) * factor * factor * mean)

    def by_pipe(choices):
        items = list(choices.items())
        out = items[-1][1]
        for p, value in items[:-1]:
            out = jnp.where(pipe == p, value, out)
        return out

    def run(enc_count):
        dec_pipes = list(range(enc_count, N_PIPE))
        top = N_PIPE - 1

        def whole(x):
            return gather_columns(
                jnp.concatenate([pick_half(x, y_hi), half_swap(pick_half(x, 1 - y_hi))], 0)
            )

        needed = jnp.where(pipe == 0, cut(enc_in), cut(dec_in))
        if enc_count < top:
            needed = jnp.where(pipe == top, cut(out_grad), needed)
        started = whole(needed)
        enc_full = started
        dec_full = started
        grad = started if enc_count < top else whole(cut(out_grad))
        outs = {}
        saved = {}
        for s in range(enc_count):
            m_in, factor = row_norm(enc_full)
            own = cut(enc_full)
            keys, k_head, values, pair_all = make_keys(m_in)
            queries, q_head = head_norm(project(m_in, query_map))
            attended = attend(queries, pair_all)
            saved[s] = (
                own, factor, queries, q_head, keys, k_head, values, pair_all, attended,
            )
            branch = reduce_columns(project(jnp.concatenate(attended, 1), out_map))
            updated = (own.astype(F32) + branch).astype(BF)
            outs[s] = updated
            if s + 1 < enc_count:
                enc_full = shift_columns(updated, 1)
        last = enc_count - 1
        sent = {p: pipe_send(outs[last], p - last) for p in dec_pipes}
        enc_piece = by_pipe(sent)
        enc_full = gather_columns(enc_piece)
        m_in, m_factor = row_norm(enc_full)
        keys, k_head, values, pair_all = make_keys(m_in)
        for s in dec_pipes:
            q_in, factor = row_norm(dec_full)
            own = cut(dec_full)
            queries, q_head = head_norm(project(q_in, query_map))
            attended = attend(queries, pair_all)
            saved[s] = (own, factor, queries, q_head, attended)
            branch = reduce_columns(project(jnp.concatenate(attended, 1), out_map))
            updated = (own.astype(F32) + branch).astype(BF)
            outs[s] = updated
            if s + 1 < N_PIPE:
                dec_full = shift_columns(updated, 1)
        dec_grads = {}
        enc_grads = {}
        kept = {}
        for s in reversed(dec_pipes):
            own, factor, queries, q_head, attended = saved[s]
            d_att, d_scores, portion_low, q_grad, stat = query_back(
                grad, queries, q_head, pair_all, attended
            )
            kept[s] = (d_att, d_scores, portion_low, queries)
            stat = reduce_stat(stat)
            d_own = reduce_columns(times_t(q_grad, query_map))
            back_q = norm_back(own, factor, d_own, stat)
            new_grad = (cut(grad).astype(F32) + back_q).astype(BF)
            dec_grads[s] = new_grad
            if s > enc_count:
                grad = shift_columns(new_grad, -1)
        d_att = by_pipe({s: kept[s][0] for s in dec_pipes})
        d_scores, portion_low, queries = (
            [by_pipe({s: kept[s][i][h] for s in dec_pipes}) for h in range(heads)]
            for i in (1, 2, 3)
        )
        d_values, k_grad, stat = key_back(
            d_att, d_scores, portion_low, queries, keys, k_head, values
        )
        stat = reduce_stat(stat)
        d_own = reduce_columns(times_t(k_grad, key_map) + times_t(d_values, value_map))
        back_m = norm_back(enc_piece, m_factor, d_own, stat)
        back_low = back_m.astype(BF)
        total = jnp.where(pipe >= enc_count, back_m, 0.0)
        for by in range(1, N_PIPE - enc_count + 1):
            valid = (pipe + by < N_PIPE) & (pipe + by >= enc_count)
            total = total + jnp.where(valid, pipe_send(back_low, -by).astype(F32), 0.0)
        total = total.astype(BF)
        for s in dec_pipes:
            enc_grads[s] = total
        grad = gather_columns(total)
        for p in range(enc_count):
            dec_grads[p] = pipe_send(dec_grads[enc_count], p - enc_count)
        for s in reversed(range(enc_count)):
            own, factor, queries, q_head, keys, k_head, values, pair_all, attended = saved[s]
            d_att, d_scores, portion_low, q_grad, stat = query_back(
                grad, queries, q_head, pair_all, attended
            )
            d_values, k_grad, k_stat = key_back(
                d_att, d_scores, portion_low, queries, keys, k_head, values
            )
            stat = reduce_stat(stat + k_stat)
            partial = (
                times_t(q_grad, query_map)
                + times_t(k_grad, key_map)
                + times_t(d_values, value_map)
            )
            d_own = reduce_columns(partial)
            back = norm_back(own, factor, d_own, stat)
            new_grad = (cut(grad).astype(F32) + back).astype(BF)
            enc_grads[s] = new_grad
            if s > 0:
                grad = shift_columns(new_grad, -1)

        def finish(choices):
            own = by_pipe(choices)
            keep = own[:tok]
            got = half_swap(own[tok:])
            return jnp.stack([jnp.where(y_hi == 0, keep, got), jnp.where(y_hi == 0, got, keep)])

        section_out = finish(outs)[None]
        section_grad = jnp.stack([finish(enc_grads), finish(dec_grads)])[None]
        return section_out, section_grad

    which = jnp.clip(enc_sections[0] - 1, 0, N_PIPE - 2)
    return lax.switch(which, [lambda n=n: run(n) for n in range(1, N_PIPE)])


def solution(mesh):
    return jax.shard_map(
        per_device,
        mesh=mesh,
        in_specs=(
            P(None, "seq", None),
            P(None, "seq", None),
            P(),
            P(),
            P("pipe", None),
            P("pipe", None, "mp"),
            P("pipe", None, "mp"),
            P("pipe", None, "mp"),
            P("pipe", "mp", None),
            P(None, "seq", None),
        ),
        out_specs=(P("pipe", None, "seq", "mp"), P("pipe", None, None, "seq", "mp")),
        check_vma=False,
    )
```

```python
import jax
import jax.numpy as jnp
from jax import lax
from jax.sharding import PartitionSpec as P

HEADS = 8
HS = 256
epsilon = 1e-06
N_PIPE = 4
N_Z = 4
BF = jnp.bfloat16
F32 = jnp.float32


def pipe_send(x, by, flip_y=0):
    pairs = []
    for p in range(N_PIPE):
        for place in range(4):
            pairs.append((p * 4 + place, ((p + by) % N_PIPE) * 4 + (place ^ (2 * flip_y))))
    return lax.ppermute(x, ("pipe", "mp"), pairs)


def core_swap(x):
    return lax.ppermute(x, "mp", [(i, i ^ 1) for i in range(4)])


def chip_swap(x):
    return lax.ppermute(x, "mp", [(i, i ^ 2) for i in range(4)])


def z_send(x, by):
    return lax.ppermute(x, "seq", [(i, (i + 2 * by) % (2 * N_Z)) for i in range(2 * N_Z)])


def half_swap(x):
    return lax.ppermute(x, "seq", [(i, i ^ 1) for i in range(2 * N_Z)])


def per_device(
    enc_in,
    dec_in,
    doc_ids,
    enc_sections,
    norm_gain,
    q_weight,
    k_weight,
    v_weight,
    o_weight,
    out_grad,
):
    pipe = lax.axis_index("pipe")
    mp = lax.axis_index("mp")
    seq = lax.axis_index("seq")
    y_lo = mp // 2
    core = mp % 2
    z = seq // 2
    y_hi = seq % 2
    tok = enc_in.shape[1]
    width = enc_in.shape[2]
    rows = 2 * tok
    share = width // 4
    heads = HEADS // 4
    head_width = heads * HS
    scale = HS ** (-0.5)
    gain = norm_gain[0]
    query_map = q_weight[0]
    key_map = k_weight[0]
    value_map = v_weight[0]
    out_map = o_weight[0]

    def cut(x):
        return lax.dynamic_slice_in_dim(x, mp * share, share, x.ndim - 1)

    gain_own = cut(gain)

    def pick_half(x, which):
        return lax.dynamic_index_in_dim(x, which, 0, keepdims=False)

    doc_row = pick_half(doc_ids, y_hi)

    def block_docs(z_from):
        first = lax.dynamic_slice_in_dim(doc_row, (z_from * 2 + y_hi) * tok, tok)
        second = lax.dynamic_slice_in_dim(doc_row, (z_from * 2 + 1 - y_hi) * tok, tok)
        return jnp.concatenate([first, second])

    key_docs = jnp.concatenate([block_docs((z - r) % N_Z) for r in range(N_Z)])
    same_doc = key_docs[:rows, None] == key_docs[None, :]

    def order_columns(a, b, ra, rb):
        low_y = y_lo == 0
        low_c = core == 0
        m0, m1 = jnp.where(low_y, a, b), jnp.where(low_y, b, a)
        s0, s1 = jnp.where(low_y, ra, rb), jnp.where(low_y, rb, ra)
        return jnp.concatenate(
            [
                jnp.where(low_c, m0, s0),
                jnp.where(low_c, s0, m0),
                jnp.where(low_c, m1, s1),
                jnp.where(low_c, s1, m1),
            ],
            1,
        )

    def gather_columns(a):
        b = chip_swap(a)
        ra = core_swap(a)
        rb = core_swap(b)
        return order_columns(a, b, ra, rb)

    def shift_columns(x, by):
        a = pipe_send(x, by)
        b = pipe_send(x, by, 1)
        ra = core_swap(a)
        rb = core_swap(b)
        return order_columns(a, b, ra, rb)

    def reduce_columns(partial):
        low = partial.astype(BF)
        first = jnp.concatenate([low[:, :share], low[:, 2 * share : 3 * share]], 1)
        second = jnp.concatenate([low[:, share : 2 * share], low[:, 3 * share :]], 1)
        keep = jnp.where(core == 0, first, second)
        away = jnp.where(core == 0, second, first)
        both = keep.astype(F32) + core_swap(away).astype(F32)
        mine = jnp.where(y_lo == 0, both[:, :share], both[:, share:])
        away = jnp.where(y_lo == 0, both[:, share:], both[:, :share]).astype(BF)
        return mine + chip_swap(away).astype(F32)

    def reduce_stat(stat):
        stat = stat + core_swap(stat)
        return stat + chip_swap(stat)

    def row_norm(x):
        values = x.astype(F32)
        factor = lax.rsqrt(jnp.mean(values * values, axis=-1, keepdims=True) + epsilon)
        return (values * factor * gain).astype(BF), factor

    def head(x, h):
        return x[:, h * HS : (h + 1) * HS]

    def head_norm(projected):
        normed, factors = [], []
        for h in range(heads):
            part = head(projected, h)
            factor = lax.rsqrt(jnp.mean(part * part, axis=-1, keepdims=True) + epsilon)
            normed.append((part * factor).astype(BF))
            factors.append(factor)
        return normed, factors

    def head_back(normed, factor, incoming):
        values = normed.astype(F32)
        return factor * (incoming - values * jnp.mean(incoming * values, axis=-1, keepdims=True))

    def project(x, weight):
        return jnp.dot(x, weight, preferred_element_type=F32)

    def times_t(x, y):
        return lax.dot_general(x, y, (((1,), (1,)), ((), ())), preferred_element_type=F32)

    def t_times(x, y):
        return lax.dot_general(x, y, (((0,), (0,)), ((), ())), preferred_element_type=F32)

    def make_keys(m_in):
        keys, k_head = head_norm(project(m_in, key_map))
        values = project(m_in, value_map).astype(BF)
        pair = jnp.concatenate(keys + [values], 1)
        blocks = {r: z_send(pair, r) for r in (2, 1, 3)}
        pair_all = jnp.concatenate([pair, blocks[1], blocks[2], blocks[3]], 0)
        return keys, k_head, values, pair_all

    def swap_rows(x):
        low, high = x[:tok], x[tok:]
        keep = jnp.where(y_hi == 0, low, high)
        return jnp.concatenate([keep, half_swap(jnp.where(y_hi == 0, high, low))], 0)

    def after(values, *first):
        return lax.optimization_barrier((values, first))[0]

    def weigh(queries, pair_all):
        out = []
        for h in range(heads):
            scores = times_t(queries[h], head(pair_all, h)) * scale
            weights = jnp.where(same_doc, jnp.exp(scores), 0.0)
            out.append((weights, jnp.sum(weights, axis=-1, keepdims=True)))
        return out

    def attend(queries, pair_all):
        attended = []
        weighed = weigh(queries, pair_all)
        for h, (weights, totals) in enumerate(weighed):
            summed = project(weights.astype(BF), head(pair_all, heads + h))
            attended.append((summed / totals).astype(BF))
        return attended

    def query_back(d_att, queries, q_head, pair_all, attended):
        d_scores, q_grad, portion_low, stat = [], [], [], 0.0
        for h, (weights, totals) in enumerate(weigh(queries, pair_all)):
            portion = weights / totals
            d_h = head(d_att, h)
            along = times_t(d_h, head(pair_all, heads + h))
            delta = jnp.sum(
                d_h.astype(F32) * attended[h].astype(F32), axis=-1, keepdims=True
            )
            d_s = (portion * (along - delta)).astype(BF)
            d_q = project(d_s, head(pair_all, h)) * scale
            grad_h = head_back(queries[h], q_head[h], d_q).astype(BF)
            stat = stat + jnp.sum(
                grad_h.astype(F32) * queries[h].astype(F32), axis=-1
            ) / q_head[h][:, 0]
            d_scores.append(d_s)
            q_grad.append(grad_h)
            portion_low.append(portion.astype(BF))
        return d_scores, portion_low, jnp.concatenate(q_grad, 1), stat

    def key_back(d_att, d_scores, portion_low, queries, keys, k_head, values):
        both = jnp.concatenate(
            [t_times(d_scores[h], queries[h]) * scale for h in range(heads)]
            + [t_times(portion_low[h], head(d_att, h)) for h in range(heads)],
            1,
        )
        low = both.astype(BF)
        got = {r: z_send(low[r * rows : (r + 1) * rows], N_Z - r) for r in (2, 1, 3)}
        total = both[:rows] + sum(got[r].astype(F32) for r in (1, 2, 3))
        d_values = total[:, head_width:].astype(BF)
        k_grad, stat = [], jnp.sum(d_values.astype(F32) * values.astype(F32), axis=-1)
        for h in range(heads):
            grad_h = head_back(keys[h], k_head[h], head(total, h)).astype(BF)
            stat = stat + jnp.sum(
                grad_h.astype(F32) * keys[h].astype(F32), axis=-1
            ) / k_head[h][:, 0]
            k_grad.append(grad_h)
        return d_values, jnp.concatenate(k_grad, 1), stat

    def norm_back(own, factor, d_own, stat):
        mean = (stat / width)[:, None] / factor
        return factor * (gain_own * d_own - own.astype(F32) * factor * factor * mean)

    def by_pipe(choices):
        items = list(choices.items())
        out = items[-1][1]
        for p, value in items[:-1]:
            out = jnp.where(pipe == p, value, out)
        return out

    def run(enc_count):
        dec_pipes = list(range(enc_count, N_PIPE))
        top = N_PIPE - 1

        def finish(own):
            keep = own[:tok]
            got = half_swap(own[tok:])
            return jnp.stack([jnp.where(y_hi == 0, keep, got), jnp.where(y_hi == 0, got, keep)])

        needed = jnp.where(pipe == 0, enc_in, dec_in)
        if enc_count < top:
            needed = jnp.where(pipe == top, out_grad, needed)
        keep_rows = jnp.where(y_hi == 0, needed[0], needed[1])
        send_rows = jnp.where(y_hi == 0, cut(needed[1]), cut(needed[0]))
        started = jnp.concatenate([keep_rows, gather_columns(half_swap(send_rows))], 0)
        enc_full = started
        dec_full = started
        outs = {}
        saved = {}
        for s in range(enc_count):
            m_in, factor = row_norm(enc_full)
            own = cut(enc_full)
            keys, k_head, values, pair_all = make_keys(m_in)
            queries, q_head = head_norm(project(m_in, query_map))
            attended = attend(queries, pair_all)
            saved[s] = (
                own, factor, queries, q_head, keys, k_head, values, pair_all, attended,
            )
            branch = reduce_columns(project(jnp.concatenate(attended, 1), out_map))
            updated = (own.astype(F32) + branch).astype(BF)
            outs[s] = updated
            if s + 1 < enc_count:
                enc_full = shift_columns(updated, 1)
        last = enc_count - 1
        if len(dec_pipes) == 1:
            enc_full = shift_columns(outs[last], 1)
        else:
            enc_full = gather_columns(
                by_pipe({p: pipe_send(outs[last], p - last) for p in dec_pipes})
            )
        enc_own = cut(enc_full)
        if enc_count < top:
            grad = started
        else:
            top_rows = after(out_grad.reshape(rows, width), enc_full)
            d_att_top = swap_rows(times_t(top_rows, out_map).astype(BF))
            grad_top = swap_rows(cut(top_rows))
        m_in, m_factor = row_norm(enc_full)
        keys, k_head, values, pair_all = make_keys(m_in)
        for s in dec_pipes:
            q_in, factor = row_norm(dec_full)
            own = cut(dec_full)
            queries, q_head = head_norm(project(q_in, query_map))
            attended = attend(queries, pair_all)
            saved[s] = (own, factor, queries, q_head, attended)
            if s < top:
                branch = reduce_columns(project(jnp.concatenate(attended, 1), out_map))
                updated = (own.astype(F32) + branch).astype(BF)
                outs[s] = updated
                dec_full = shift_columns(updated, 1)
        dec_grads = {}
        enc_grads = {}
        kept = {}
        for s in reversed(dec_pipes):
            own, factor, queries, q_head, attended = saved[s]
            if s == top and enc_count == top:
                d_att, grad_own = d_att_top, grad_top
            else:
                d_att, grad_own = times_t(grad, out_map).astype(BF), cut(grad)
            d_scores, portion_low, q_grad, stat = query_back(
                d_att, queries, q_head, pair_all, attended
            )
            kept[s] = (d_att, d_scores, portion_low, queries)
            stat = reduce_stat(stat)
            d_own = reduce_columns(times_t(q_grad, query_map))
            back_q = norm_back(own, factor, d_own, stat)
            new_grad = (grad_own.astype(F32) + back_q).astype(BF)
            dec_grads[s] = new_grad
            if s > enc_count:
                grad = shift_columns(new_grad, -1)
        d_att = by_pipe({s: kept[s][0] for s in dec_pipes})
        d_scores, portion_low, queries = (
            [by_pipe({s: kept[s][i][h] for s in dec_pipes}) for h in range(heads)]
            for i in (1, 2, 3)
        )
        d_values, k_grad, stat = key_back(
            d_att, d_scores, portion_low, queries, keys, k_head, values
        )
        stat = reduce_stat(stat)
        for p in range(enc_count):
            dec_grads[p] = pipe_send(dec_grads[enc_count], p - enc_count)
        done = by_pipe(dec_grads)
        d_own = reduce_columns(times_t(k_grad, key_map) + times_t(d_values, value_map))
        d_own, done = lax.optimization_barrier((d_own, done))
        back_m = norm_back(enc_own, m_factor, d_own, stat)
        back_low = back_m.astype(BF)
        if len(dec_pipes) == 1:
            total = back_low
            grad = shift_columns(total, -1)
        else:
            total = jnp.where(pipe >= enc_count, back_m, 0.0)
            for by in range(1, N_PIPE - enc_count + 1):
                valid = (pipe + by < N_PIPE) & (pipe + by >= enc_count)
                total = total + jnp.where(valid, pipe_send(back_low, -by).astype(F32), 0.0)
            total = total.astype(BF)
            grad = gather_columns(total)
        for s in dec_pipes:
            enc_grads[s] = total
        attended = after(saved[top][4], total)
        branch = reduce_columns(project(jnp.concatenate(attended, 1), out_map))
        outs[top] = (saved[top][0].astype(F32) + branch).astype(BF)
        for s in reversed(range(enc_count)):
            own, factor, queries, q_head, keys, k_head, values, pair_all, attended = saved[s]
            d_att = times_t(grad, out_map).astype(BF)
            if s == last:
                done = finish(after(done, d_att))
            if s == 0:
                section_out = finish(after(by_pipe(outs), d_att))[None]
            d_scores, portion_low, q_grad, stat = query_back(
                d_att, queries, q_head, pair_all, attended
            )
            d_values, k_grad, k_stat = key_back(
                d_att, d_scores, portion_low, queries, keys, k_head, values
            )
            if s == last:
                k_grad, done = lax.optimization_barrier((k_grad, done))
            if s == 0:
                k_grad, section_out = lax.optimization_barrier((k_grad, section_out))
            stat = reduce_stat(stat + k_stat)
            partial = (
                times_t(q_grad, query_map)
                + times_t(k_grad, key_map)
                + times_t(d_values, value_map)
            )
            d_own = reduce_columns(partial)
            back = norm_back(own, factor, d_own, stat)
            new_grad = (cut(grad).astype(F32) + back).astype(BF)
            enc_grads[s] = new_grad
            if s > 0:
                grad = shift_columns(new_grad, -1)

        section_grad = jnp.stack([finish(by_pipe(enc_grads)), done])[None]
        return section_out, section_grad

    which = jnp.clip(enc_sections[0] - 1, 0, N_PIPE - 2)
    return lax.switch(which, [lambda n=n: run(n) for n in range(1, N_PIPE)])


def solution(mesh):
    return jax.shard_map(
        per_device,
        mesh=mesh,
        in_specs=(
            P(None, "seq", None),
            P(None, "seq", None),
            P(),
            P(),
            P("pipe", None),
            P("pipe", None, "mp"),
            P("pipe", None, "mp"),
            P("pipe", None, "mp"),
            P("pipe", "mp", None),
            P(None, "seq", None),
        ),
        out_specs=(P("pipe", None, "seq", "mp"), P("pipe", None, None, "seq", "mp")),
        check_vma=False,
    )
```

```python
import jax
import jax.numpy as jnp
from jax import lax
from jax.sharding import PartitionSpec as P

HEADS = 8
HS = 256
epsilon = 1e-06
N_PIPE = 4
N_Z = 4
BF = jnp.bfloat16
F32 = jnp.float32


def pipe_send(x, by, flip_y=0):
    pairs = []
    for p in range(N_PIPE):
        for place in range(4):
            pairs.append((p * 4 + place, ((p + by) % N_PIPE) * 4 + (place ^ (2 * flip_y))))
    return lax.ppermute(x, ("pipe", "mp"), pairs)


def core_swap(x):
    return lax.ppermute(x, "mp", [(i, i ^ 1) for i in range(4)])


def chip_swap(x):
    return lax.ppermute(x, "mp", [(i, i ^ 2) for i in range(4)])


def z_send(x, by):
    return lax.ppermute(x, "seq", [(i, (i + 2 * by) % (2 * N_Z)) for i in range(2 * N_Z)])


def half_swap(x):
    return lax.ppermute(x, "seq", [(i, i ^ 1) for i in range(2 * N_Z)])


def per_device(
    enc_in,
    dec_in,
    doc_ids,
    enc_sections,
    norm_gain,
    q_weight,
    k_weight,
    v_weight,
    o_weight,
    out_grad,
):
    pipe = lax.axis_index("pipe")
    mp = lax.axis_index("mp")
    seq = lax.axis_index("seq")
    y_lo = mp // 2
    core = mp % 2
    z = seq // 2
    y_hi = seq % 2
    tok = enc_in.shape[1]
    width = enc_in.shape[2]
    rows = 2 * tok
    share = width // 4
    heads = HEADS // 4
    head_width = heads * HS
    scale = HS ** (-0.5)
    gain = norm_gain[0]
    query_map = q_weight[0]
    key_map = k_weight[0]
    value_map = v_weight[0]
    out_map = o_weight[0]

    def cut(x):
        return lax.dynamic_slice_in_dim(x, mp * share, share, x.ndim - 1)

    gain_own = cut(gain)

    def pick_half(x, which):
        return lax.dynamic_index_in_dim(x, which, 0, keepdims=False)

    doc_row = pick_half(doc_ids, y_hi)

    def block_docs(z_from):
        first = lax.dynamic_slice_in_dim(doc_row, (z_from * 2 + y_hi) * tok, tok)
        second = lax.dynamic_slice_in_dim(doc_row, (z_from * 2 + 1 - y_hi) * tok, tok)
        return jnp.concatenate([first, second])

    key_docs = jnp.concatenate([block_docs((z - r) % N_Z) for r in range(N_Z)])
    same_doc = key_docs[:rows, None] == key_docs[None, :]

    def order_columns(a, b, ra, rb):
        low_y = y_lo == 0
        low_c = core == 0
        m0, m1 = jnp.where(low_y, a, b), jnp.where(low_y, b, a)
        s0, s1 = jnp.where(low_y, ra, rb), jnp.where(low_y, rb, ra)
        return jnp.concatenate(
            [
                jnp.where(low_c, m0, s0),
                jnp.where(low_c, s0, m0),
                jnp.where(low_c, m1, s1),
                jnp.where(low_c, s1, m1),
            ],
            1,
        )

    def gather_columns(a):
        b = chip_swap(a)
        ra = core_swap(a)
        rb = core_swap(b)
        return order_columns(a, b, ra, rb)

    def shift_columns(x, by):
        first = pipe_send(x[:tok], by)
        other_second = pipe_send(x[tok:], by, 1)
        second = pipe_send(x[tok:], by)
        a = jnp.concatenate([first, second], 0)
        b = jnp.concatenate([chip_swap(first), other_second], 0)
        return order_columns(a, b, core_swap(a), core_swap(b))

    def reduce_columns(partial):
        low = partial.astype(BF)
        first = jnp.concatenate([low[:, :share], low[:, 2 * share : 3 * share]], 1)
        second = jnp.concatenate([low[:, share : 2 * share], low[:, 3 * share :]], 1)
        keep = jnp.where(core == 0, first, second)
        away = jnp.where(core == 0, second, first)
        both = keep.astype(F32) + core_swap(away).astype(F32)
        mine = jnp.where(y_lo == 0, both[:, :share], both[:, share:])
        away = jnp.where(y_lo == 0, both[:, share:], both[:, :share]).astype(BF)
        return mine + chip_swap(away).astype(F32)

    def reduce_stat(stat):
        stat = stat + core_swap(stat)
        return stat + chip_swap(stat)

    def row_norm(x):
        values = x.astype(F32)
        factor = lax.rsqrt(jnp.mean(values * values, axis=-1, keepdims=True) + epsilon)
        return (values * factor * gain).astype(BF), factor

    def head(x, h):
        return x[:, h * HS : (h + 1) * HS]

    def head_norm(projected):
        normed, factors = [], []
        for h in range(heads):
            part = head(projected, h)
            factor = lax.rsqrt(jnp.mean(part * part, axis=-1, keepdims=True) + epsilon)
            normed.append((part * factor).astype(BF))
            factors.append(factor)
        return normed, factors

    def head_back(normed, factor, incoming):
        values = normed.astype(F32)
        return factor * (incoming - values * jnp.mean(incoming * values, axis=-1, keepdims=True))

    def project(x, weight):
        return jnp.dot(x, weight, preferred_element_type=F32)

    def times_t(x, y):
        return lax.dot_general(x, y, (((1,), (1,)), ((), ())), preferred_element_type=F32)

    def t_times(x, y):
        return lax.dot_general(x, y, (((0,), (0,)), ((), ())), preferred_element_type=F32)

    def make_keys(m_in):
        keys, k_head = head_norm(project(m_in, key_map))
        values = project(m_in, value_map).astype(BF)
        pair = jnp.concatenate(keys + [values], 1)
        blocks = {r: z_send(pair, r) for r in (2, 1, 3)}
        pair_all = jnp.concatenate([pair, blocks[1], blocks[2], blocks[3]], 0)
        return keys, k_head, values, pair_all

    def swap_rows(x):
        low, high = x[:tok], x[tok:]
        keep = jnp.where(y_hi == 0, low, high)
        return jnp.concatenate([keep, half_swap(jnp.where(y_hi == 0, high, low))], 0)

    def after(values, *first):
        return lax.optimization_barrier((values, first))[0]

    def weigh(queries, pair_all):
        out = []
        for h in range(heads):
            scores = times_t(queries[h], head(pair_all, h)) * scale
            weights = jnp.where(same_doc, jnp.exp(scores), 0.0)
            out.append((weights, jnp.sum(weights, axis=-1, keepdims=True)))
        return out

    def attend(queries, pair_all):
        attended = []
        weighed = weigh(queries, pair_all)
        for h, (weights, totals) in enumerate(weighed):
            summed = project(weights.astype(BF), head(pair_all, heads + h))
            attended.append((summed / totals).astype(BF))
        return attended

    def query_back(d_att, queries, q_head, pair_all, attended):
        d_scores, q_grad, portion_low, stat = [], [], [], 0.0
        for h, (weights, totals) in enumerate(weigh(queries, pair_all)):
            portion = weights / totals
            d_h = head(d_att, h)
            along = times_t(d_h, head(pair_all, heads + h))
            delta = jnp.sum(
                d_h.astype(F32) * attended[h].astype(F32), axis=-1, keepdims=True
            )
            d_s = (portion * (along - delta)).astype(BF)
            d_q = project(d_s, head(pair_all, h)) * scale
            grad_h = head_back(queries[h], q_head[h], d_q).astype(BF)
            stat = stat + jnp.sum(
                grad_h.astype(F32) * queries[h].astype(F32), axis=-1
            ) / q_head[h][:, 0]
            d_scores.append(d_s)
            q_grad.append(grad_h)
            portion_low.append(portion.astype(BF))
        return d_scores, portion_low, jnp.concatenate(q_grad, 1), stat

    def key_back(d_att, d_scores, portion_low, queries, keys, k_head, values):
        both = jnp.concatenate(
            [t_times(d_scores[h], queries[h]) * scale for h in range(heads)]
            + [t_times(portion_low[h], head(d_att, h)) for h in range(heads)],
            1,
        )
        low = both.astype(BF)
        got = {r: z_send(low[r * rows : (r + 1) * rows], N_Z - r) for r in (2, 1, 3)}
        total = both[:rows] + sum(got[r].astype(F32) for r in (1, 2, 3))
        d_values = total[:, head_width:].astype(BF)
        k_grad, stat = [], jnp.sum(d_values.astype(F32) * values.astype(F32), axis=-1)
        for h in range(heads):
            grad_h = head_back(keys[h], k_head[h], head(total, h)).astype(BF)
            stat = stat + jnp.sum(
                grad_h.astype(F32) * keys[h].astype(F32), axis=-1
            ) / k_head[h][:, 0]
            k_grad.append(grad_h)
        return d_values, jnp.concatenate(k_grad, 1), stat

    def norm_back(own, factor, d_own, stat):
        mean = (stat / width)[:, None] / factor
        return factor * (gain_own * d_own - own.astype(F32) * factor * factor * mean)

    def by_pipe(choices):
        items = list(choices.items())
        out = items[-1][1]
        for p, value in items[:-1]:
            out = jnp.where(pipe == p, value, out)
        return out

    def run(enc_count):
        dec_pipes = list(range(enc_count, N_PIPE))
        top = N_PIPE - 1

        def finish(own):
            keep = own[:tok]
            got = half_swap(own[tok:])
            return jnp.stack([jnp.where(y_hi == 0, keep, got), jnp.where(y_hi == 0, got, keep)])

        needed = jnp.where(pipe == 0, enc_in, dec_in)
        if enc_count < top:
            needed = jnp.where(pipe == top, out_grad, needed)
        keep_rows = jnp.where(y_hi == 0, needed[0], needed[1])
        send_rows = jnp.where(y_hi == 0, cut(needed[1]), cut(needed[0]))
        started = jnp.concatenate([keep_rows, gather_columns(half_swap(send_rows))], 0)
        enc_full = started
        dec_full = started
        outs = {}
        saved = {}
        for s in range(enc_count):
            m_in, factor = row_norm(enc_full)
            own = cut(enc_full)
            keys, k_head, values, pair_all = make_keys(m_in)
            queries, q_head = head_norm(project(m_in, query_map))
            attended = attend(queries, pair_all)
            saved[s] = (
                own, factor, queries, q_head, keys, k_head, values, pair_all, attended,
            )
            branch = reduce_columns(project(jnp.concatenate(attended, 1), out_map))
            updated = (own.astype(F32) + branch).astype(BF)
            outs[s] = updated
            if s + 1 < enc_count:
                enc_full = shift_columns(updated, 1)
        last = enc_count - 1
        if len(dec_pipes) == 1:
            enc_full = shift_columns(outs[last], 1)
        else:
            enc_full = gather_columns(
                by_pipe({p: pipe_send(outs[last], p - last) for p in dec_pipes})
            )
        enc_own = cut(enc_full)
        if enc_count < top:
            grad = started
        else:
            top_rows = after(out_grad.reshape(rows, width), enc_full)
            d_att_top = swap_rows(times_t(top_rows, out_map).astype(BF))
            grad_top = swap_rows(cut(top_rows))
        m_in, m_factor = row_norm(enc_full)
        keys, k_head, values, pair_all = make_keys(m_in)
        for s in dec_pipes:
            q_in, factor = row_norm(dec_full)
            own = cut(dec_full)
            queries, q_head = head_norm(project(q_in, query_map))
            attended = attend(queries, pair_all)
            saved[s] = (own, factor, queries, q_head, attended)
            if s < top:
                branch = reduce_columns(project(jnp.concatenate(attended, 1), out_map))
                updated = (own.astype(F32) + branch).astype(BF)
                outs[s] = updated
                dec_full = shift_columns(updated, 1)
        dec_grads = {}
        enc_grads = {}
        kept = {}
        for s in reversed(dec_pipes):
            own, factor, queries, q_head, attended = saved[s]
            if s == top and enc_count == top:
                d_att, grad_own = d_att_top, grad_top
            else:
                d_att, grad_own = times_t(grad, out_map).astype(BF), cut(grad)
            d_scores, portion_low, q_grad, stat = query_back(
                d_att, queries, q_head, pair_all, attended
            )
            kept[s] = (d_att, d_scores, portion_low, queries)
            if s == enc_count:
                waiting = (own, factor, q_grad, stat, grad_own)
                break
            stat = reduce_stat(stat)
            d_own = reduce_columns(times_t(q_grad, query_map))
            back_q = norm_back(own, factor, d_own, stat)
            new_grad = (grad_own.astype(F32) + back_q).astype(BF)
            dec_grads[s] = new_grad
            grad = shift_columns(new_grad, -1)
        d_att = by_pipe({s: kept[s][0] for s in dec_pipes})
        d_scores, portion_low, queries = (
            [by_pipe({s: kept[s][i][h] for s in dec_pipes}) for h in range(heads)]
            for i in (1, 2, 3)
        )
        d_values, k_grad, stat = key_back(
            d_att, d_scores, portion_low, queries, keys, k_head, values
        )
        stat = reduce_stat(stat)
        d_own = reduce_columns(times_t(k_grad, key_map) + times_t(d_values, value_map))
        back_m = norm_back(enc_own, m_factor, d_own, stat)
        back_low = back_m.astype(BF)

        def first_back(ready):
            own, factor, q_grad, stat, grad_own = waiting
            q_grad, stat = after((q_grad, stat), ready)
            stat = reduce_stat(stat)
            d_own = reduce_columns(times_t(q_grad, query_map))
            back_q = norm_back(own, factor, d_own, stat)
            return (grad_own.astype(F32) + back_q).astype(BF)

        if len(dec_pipes) == 1:
            total = back_low
            grad = shift_columns(total, -1)
            new_grad = first_back(total)
        else:
            new_grad = first_back(back_low)
            total = jnp.where(pipe >= enc_count, back_m, 0.0)
            for by in range(1, N_PIPE - enc_count + 1):
                valid = (pipe + by < N_PIPE) & (pipe + by >= enc_count)
                total = total + jnp.where(valid, pipe_send(back_low, -by).astype(F32), 0.0)
            total, new_grad = lax.optimization_barrier((total.astype(BF), new_grad))
            grad = gather_columns(total)
        dec_grads[enc_count] = new_grad
        for s in dec_pipes:
            enc_grads[s] = total
        passed = new_grad if enc_count == top else after(new_grad, grad)
        for p in range(enc_count):
            dec_grads[p] = pipe_send(passed, p - enc_count)
        done = by_pipe(dec_grads)
        attended = after(saved[top][4], new_grad)
        branch = reduce_columns(project(jnp.concatenate(attended, 1), out_map))
        outs[top] = (saved[top][0].astype(F32) + branch).astype(BF)
        for s in reversed(range(enc_count)):
            own, factor, queries, q_head, keys, k_head, values, pair_all, attended = saved[s]
            d_att = times_t(grad, out_map).astype(BF)
            if s == last - 1:
                done = finish(after(done, d_att))
            if s == 0:
                section_out = finish(after(by_pipe(outs), d_att))[None]
            d_scores, portion_low, q_grad, stat = query_back(
                d_att, queries, q_head, pair_all, attended
            )
            d_values, k_grad, k_stat = key_back(
                d_att, d_scores, portion_low, queries, keys, k_head, values
            )
            if s == last:
                k_grad, done = lax.optimization_barrier((k_grad, done))
            if s == 0 and enc_count > 1:
                k_grad, section_out = lax.optimization_barrier((k_grad, section_out))
            stat = reduce_stat(stat + k_stat)
            partial = (
                times_t(q_grad, query_map)
                + times_t(k_grad, key_map)
                + times_t(d_values, value_map)
            )
            d_own = reduce_columns(partial)
            if s == 0:
                if enc_count == 1:
                    done = finish(done)
                d_own, done, section_out = lax.optimization_barrier((d_own, done, section_out))
            back = norm_back(own, factor, d_own, stat)
            new_grad = (cut(grad).astype(F32) + back).astype(BF)
            enc_grads[s] = new_grad
            if s > 0:
                grad = shift_columns(new_grad, -1)

        section_grad = jnp.stack([finish(by_pipe(enc_grads)), done])[None]
        return section_out, section_grad

    which = jnp.clip(enc_sections[0] - 1, 0, N_PIPE - 2)
    return lax.switch(which, [lambda n=n: run(n) for n in range(1, N_PIPE)])


def solution(mesh):
    return jax.shard_map(
        per_device,
        mesh=mesh,
        in_specs=(
            P(None, "seq", None),
            P(None, "seq", None),
            P(),
            P(),
            P("pipe", None),
            P("pipe", None, "mp"),
            P("pipe", None, "mp"),
            P("pipe", None, "mp"),
            P("pipe", "mp", None),
            P(None, "seq", None),
        ),
        out_specs=(P("pipe", None, "seq", "mp"), P("pipe", None, None, "seq", "mp")),
        check_vma=False,
    )
```

```python
import jax
import jax.numpy as jnp
from jax import lax
from jax.sharding import PartitionSpec as P

HEADS = 8
HS = 256
epsilon = 1e-06
N_PIPE = 4
N_Z = 4
BF = jnp.bfloat16
F32 = jnp.float32


def pipe_send(x, by, flip_y=0):
    pairs = []
    for p in range(N_PIPE):
        for place in range(4):
            pairs.append((p * 4 + place, ((p + by) % N_PIPE) * 4 + (place ^ (2 * flip_y))))
    return lax.ppermute(x, ("pipe", "mp"), pairs)


def core_swap(x):
    return lax.ppermute(x, "mp", [(i, i ^ 1) for i in range(4)])


def chip_swap(x):
    return lax.ppermute(x, "mp", [(i, i ^ 2) for i in range(4)])


def z_send(x, by):
    return lax.ppermute(x, "seq", [(i, (i + 2 * by) % (2 * N_Z)) for i in range(2 * N_Z)])


def half_swap(x):
    return lax.ppermute(x, "seq", [(i, i ^ 1) for i in range(2 * N_Z)])


def per_device(
    enc_in,
    dec_in,
    doc_ids,
    enc_sections,
    norm_gain,
    q_weight,
    k_weight,
    v_weight,
    o_weight,
    out_grad,
):
    pipe = lax.axis_index("pipe")
    mp = lax.axis_index("mp")
    seq = lax.axis_index("seq")
    y_lo = mp // 2
    core = mp % 2
    z = seq // 2
    y_hi = seq % 2
    tok = enc_in.shape[1]
    width = enc_in.shape[2]
    rows = 2 * tok
    share = width // 4
    heads = HEADS // 4
    head_width = heads * HS
    scale = HS ** (-0.5)
    gain = norm_gain[0]
    query_map = q_weight[0]
    key_map = k_weight[0]
    value_map = v_weight[0]
    out_map = o_weight[0]

    def cut(x):
        return lax.dynamic_slice_in_dim(x, mp * share, share, x.ndim - 1)

    gain_own = cut(gain)

    def pick_half(x, which):
        return lax.dynamic_index_in_dim(x, which, 0, keepdims=False)

    doc_row = pick_half(doc_ids, y_hi)

    def block_docs(z_from):
        first = lax.dynamic_slice_in_dim(doc_row, (z_from * 2 + y_hi) * tok, tok)
        second = lax.dynamic_slice_in_dim(doc_row, (z_from * 2 + 1 - y_hi) * tok, tok)
        return jnp.concatenate([first, second])

    key_docs = jnp.concatenate([block_docs((z - r) % N_Z) for r in range(N_Z)])
    same_doc = key_docs[:rows, None] == key_docs[None, :]

    def order_columns(a, b, ra, rb):
        low_y = y_lo == 0
        low_c = core == 0
        m0, m1 = jnp.where(low_y, a, b), jnp.where(low_y, b, a)
        s0, s1 = jnp.where(low_y, ra, rb), jnp.where(low_y, rb, ra)
        return jnp.concatenate(
            [
                jnp.where(low_c, m0, s0),
                jnp.where(low_c, s0, m0),
                jnp.where(low_c, m1, s1),
                jnp.where(low_c, s1, m1),
            ],
            1,
        )

    def gather_columns(a):
        b = chip_swap(a)
        ra = core_swap(a)
        rb = core_swap(b)
        return order_columns(a, b, ra, rb)

    def shift_columns(x, by):
        first = pipe_send(x[:tok], by)
        other_second = pipe_send(x[tok:], by, 1)
        second = pipe_send(x[tok:], by)
        a = jnp.concatenate([first, second], 0)
        b = jnp.concatenate([chip_swap(first), other_second], 0)
        return order_columns(a, b, core_swap(a), core_swap(b))

    def reduce_columns(partial):
        low = partial.astype(BF)
        first = jnp.concatenate([low[:, :share], low[:, 2 * share : 3 * share]], 1)
        second = jnp.concatenate([low[:, share : 2 * share], low[:, 3 * share :]], 1)
        keep = jnp.where(core == 0, first, second)
        away = jnp.where(core == 0, second, first)
        both = keep.astype(F32) + core_swap(away).astype(F32)
        mine = jnp.where(y_lo == 0, both[:, :share], both[:, share:])
        away = jnp.where(y_lo == 0, both[:, share:], both[:, :share]).astype(BF)
        return mine + chip_swap(away).astype(F32)

    def reduce_stat(stat):
        stat = stat + core_swap(stat)
        return stat + chip_swap(stat)

    def row_norm(x):
        values = x.astype(F32)
        factor = lax.rsqrt(jnp.mean(values * values, axis=-1, keepdims=True) + epsilon)
        return (values * factor * gain).astype(BF), factor

    def head(x, h):
        return x[:, h * HS : (h + 1) * HS]

    def head_norm(projected):
        normed, factors = [], []
        for h in range(heads):
            part = head(projected, h)
            factor = lax.rsqrt(jnp.mean(part * part, axis=-1, keepdims=True) + epsilon)
            normed.append((part * factor).astype(BF))
            factors.append(factor)
        return normed, factors

    def head_back(normed, factor, incoming):
        values = normed.astype(F32)
        return factor * (incoming - values * jnp.mean(incoming * values, axis=-1, keepdims=True))

    def project(x, weight):
        return jnp.dot(x, weight, preferred_element_type=F32)

    def times_t(x, y):
        return lax.dot_general(x, y, (((1,), (1,)), ((), ())), preferred_element_type=F32)

    def t_times(x, y):
        return lax.dot_general(x, y, (((0,), (0,)), ((), ())), preferred_element_type=F32)

    def make_keys(m_in):
        keys, k_head = head_norm(project(m_in, key_map))
        values = project(m_in, value_map).astype(BF)
        pair = jnp.concatenate(keys + [values], 1)
        blocks = {r: z_send(pair, r) for r in (1, 3, 2)}
        pair_all = jnp.concatenate([pair, blocks[1], blocks[2], blocks[3]], 0)
        return keys, k_head, values, pair_all

    def swap_rows(x):
        low, high = x[:tok], x[tok:]
        keep = jnp.where(y_hi == 0, low, high)
        return jnp.concatenate([keep, half_swap(jnp.where(y_hi == 0, high, low))], 0)

    def after(values, *first):
        return lax.optimization_barrier((values, first))[0]

    def weigh(queries, pair_all):
        out = []
        for h in range(heads):
            scores = times_t(queries[h], head(pair_all, h)) * scale
            weights = jnp.where(same_doc, jnp.exp(scores), 0.0)
            out.append((weights, jnp.sum(weights, axis=-1, keepdims=True)))
        return out

    def attend(queries, pair_all):
        attended = []
        weighed = weigh(queries, pair_all)
        for h, (weights, totals) in enumerate(weighed):
            summed = project(weights.astype(BF), head(pair_all, heads + h))
            attended.append((summed / totals).astype(BF))
        return attended

    def query_back(d_att, queries, q_head, pair_all, attended):
        d_scores, q_grad, portion_low, stat = [], [], [], 0.0
        for h, (weights, totals) in enumerate(weigh(queries, pair_all)):
            portion = weights / totals
            d_h = head(d_att, h)
            along = times_t(d_h, head(pair_all, heads + h))
            delta = jnp.sum(
                d_h.astype(F32) * attended[h].astype(F32), axis=-1, keepdims=True
            )
            d_s = (portion * (along - delta)).astype(BF)
            d_q = project(d_s, head(pair_all, h)) * scale
            grad_h = head_back(queries[h], q_head[h], d_q).astype(BF)
            stat = stat + jnp.sum(
                grad_h.astype(F32) * queries[h].astype(F32), axis=-1
            ) / q_head[h][:, 0]
            d_scores.append(d_s)
            q_grad.append(grad_h)
            portion_low.append(portion.astype(BF))
        return d_scores, portion_low, jnp.concatenate(q_grad, 1), stat

    def key_back(d_att, d_scores, portion_low, queries, keys, k_head, values):
        both = jnp.concatenate(
            [t_times(d_scores[h], queries[h]) * scale for h in range(heads)]
            + [t_times(portion_low[h], head(d_att, h)) for h in range(heads)],
            1,
        )
        low = both.astype(BF)
        got = {r: z_send(low[r * rows : (r + 1) * rows], N_Z - r) for r in (1, 3, 2)}
        total = both[:rows] + sum(got[r].astype(F32) for r in (1, 2, 3))
        d_values = total[:, head_width:].astype(BF)
        k_grad, stat = [], jnp.sum(d_values.astype(F32) * values.astype(F32), axis=-1)
        for h in range(heads):
            grad_h = head_back(keys[h], k_head[h], head(total, h)).astype(BF)
            stat = stat + jnp.sum(
                grad_h.astype(F32) * keys[h].astype(F32), axis=-1
            ) / k_head[h][:, 0]
            k_grad.append(grad_h)
        return d_values, jnp.concatenate(k_grad, 1), stat

    def norm_back(own, factor, d_own, stat):
        mean = (stat / width)[:, None] / factor
        return factor * (gain_own * d_own - own.astype(F32) * factor * factor * mean)

    def by_pipe(choices):
        items = list(choices.items())
        out = items[-1][1]
        for p, value in items[:-1]:
            out = jnp.where(pipe == p, value, out)
        return out

    def run(enc_count):
        dec_pipes = list(range(enc_count, N_PIPE))
        top = N_PIPE - 1

        def finish(own):
            keep = own[:tok]
            got = half_swap(own[tok:])
            return jnp.stack([jnp.where(y_hi == 0, keep, got), jnp.where(y_hi == 0, got, keep)])

        needed = jnp.where(pipe == 0, enc_in, dec_in)
        if enc_count < top:
            needed = jnp.where(pipe == top, out_grad, needed)
        keep_rows = jnp.where(y_hi == 0, needed[0], needed[1])
        send_rows = jnp.where(y_hi == 0, cut(needed[1]), cut(needed[0]))
        started = jnp.concatenate([keep_rows, gather_columns(half_swap(send_rows))], 0)
        enc_full = started
        dec_full = started
        outs = {}
        saved = {}
        for s in range(enc_count):
            m_in, factor = row_norm(enc_full)
            own = cut(enc_full)
            keys, k_head, values, pair_all = make_keys(m_in)
            queries, q_head = head_norm(project(m_in, query_map))
            attended = attend(queries, pair_all)
            saved[s] = (
                own, factor, queries, q_head, keys, k_head, values, pair_all, attended,
            )
            branch = reduce_columns(project(jnp.concatenate(attended, 1), out_map))
            updated = (own.astype(F32) + branch).astype(BF)
            outs[s] = updated
            if s + 1 < enc_count:
                enc_full = shift_columns(updated, 1)
        last = enc_count - 1
        if len(dec_pipes) == 1:
            enc_full = shift_columns(outs[last], 1)
        else:
            enc_full = gather_columns(
                by_pipe({p: pipe_send(outs[last], p - last) for p in dec_pipes})
            )
        enc_own = cut(enc_full)
        if enc_count < top:
            grad = started
        else:
            top_rows = after(out_grad.reshape(rows, width), enc_full)
            d_att_top = swap_rows(times_t(top_rows, out_map).astype(BF))
            grad_top = swap_rows(cut(top_rows))
        m_in, m_factor = row_norm(enc_full)
        keys, k_head, values, pair_all = make_keys(m_in)
        for s in dec_pipes:
            q_in, factor = row_norm(dec_full)
            own = cut(dec_full)
            queries, q_head = head_norm(project(q_in, query_map))
            attended = attend(queries, pair_all)
            saved[s] = (own, factor, queries, q_head, attended)
            if s < top:
                branch = reduce_columns(project(jnp.concatenate(attended, 1), out_map))
                updated = (own.astype(F32) + branch).astype(BF)
                outs[s] = updated
                dec_full = shift_columns(updated, 1)
        dec_grads = {}
        enc_grads = {}
        kept = {}
        for s in reversed(dec_pipes):
            own, factor, queries, q_head, attended = saved[s]
            if s == top and enc_count == top:
                d_att, grad_own = d_att_top, grad_top
            else:
                d_att, grad_own = times_t(grad, out_map).astype(BF), cut(grad)
            d_scores, portion_low, q_grad, stat = query_back(
                d_att, queries, q_head, pair_all, attended
            )
            kept[s] = (d_att, d_scores, portion_low, queries)
            if s == enc_count:
                waiting = (own, factor, q_grad, stat, grad_own)
                break
            stat = reduce_stat(stat)
            d_own = reduce_columns(times_t(q_grad, query_map))
            back_q = norm_back(own, factor, d_own, stat)
            new_grad = (grad_own.astype(F32) + back_q).astype(BF)
            dec_grads[s] = new_grad
            grad = shift_columns(new_grad, -1)
        d_att = by_pipe({s: kept[s][0] for s in dec_pipes})
        d_scores, portion_low, queries = (
            [by_pipe({s: kept[s][i][h] for s in dec_pipes}) for h in range(heads)]
            for i in (1, 2, 3)
        )
        d_values, k_grad, stat = key_back(
            d_att, d_scores, portion_low, queries, keys, k_head, values
        )
        stat = reduce_stat(stat)
        d_own = reduce_columns(times_t(k_grad, key_map) + times_t(d_values, value_map))
        back_m = norm_back(enc_own, m_factor, d_own, stat)
        back_low = back_m.astype(BF)

        def first_back(ready):
            own, factor, q_grad, stat, grad_own = waiting
            q_grad, stat = after((q_grad, stat), ready)
            stat = reduce_stat(stat)
            d_own = reduce_columns(times_t(q_grad, query_map))
            back_q = norm_back(own, factor, d_own, stat)
            return (grad_own.astype(F32) + back_q).astype(BF)

        if len(dec_pipes) == 1:
            total = back_low
            grad = shift_columns(total, -1)
            new_grad = first_back(total)
        else:
            new_grad = first_back(back_low)
            total = jnp.where(pipe >= enc_count, back_m, 0.0)
            for by in range(1, N_PIPE - enc_count + 1):
                valid = (pipe + by < N_PIPE) & (pipe + by >= enc_count)
                total = total + jnp.where(valid, pipe_send(back_low, -by).astype(F32), 0.0)
            total, new_grad = lax.optimization_barrier((total.astype(BF), new_grad))
            grad = gather_columns(total)
        dec_grads[enc_count] = new_grad
        for s in dec_pipes:
            enc_grads[s] = total
        passed = new_grad if enc_count == top else after(new_grad, grad)
        for p in range(enc_count):
            dec_grads[p] = pipe_send(passed, p - enc_count)
        done = by_pipe(dec_grads)
        attended = after(saved[top][4], new_grad)
        branch = reduce_columns(project(jnp.concatenate(attended, 1), out_map))
        outs[top] = (saved[top][0].astype(F32) + branch).astype(BF)
        for s in reversed(range(enc_count)):
            own, factor, queries, q_head, keys, k_head, values, pair_all, attended = saved[s]
            d_att = times_t(grad, out_map).astype(BF)
            if s == last - 1:
                done = finish(after(done, d_att))
            if s == 0:
                section_out = finish(after(by_pipe(outs), d_att))[None]
            d_scores, portion_low, q_grad, stat = query_back(
                d_att, queries, q_head, pair_all, attended
            )
            d_values, k_grad, k_stat = key_back(
                d_att, d_scores, portion_low, queries, keys, k_head, values
            )
            if s == last:
                k_grad, done = lax.optimization_barrier((k_grad, done))
            if s == 0 and enc_count > 1:
                k_grad, section_out = lax.optimization_barrier((k_grad, section_out))
            stat = reduce_stat(stat + k_stat)
            partial = (
                times_t(q_grad, query_map)
                + times_t(k_grad, key_map)
                + times_t(d_values, value_map)
            )
            d_own = reduce_columns(partial)
            if s == 0:
                if enc_count == 1:
                    done = finish(done)
                d_own, done, section_out = lax.optimization_barrier((d_own, done, section_out))
            back = norm_back(own, factor, d_own, stat)
            new_grad = (cut(grad).astype(F32) + back).astype(BF)
            enc_grads[s] = new_grad
            if s > 0:
                grad = shift_columns(new_grad, -1)

        section_grad = jnp.stack([finish(by_pipe(enc_grads)), done])[None]
        return section_out, section_grad

    which = jnp.clip(enc_sections[0] - 1, 0, N_PIPE - 2)
    return lax.switch(which, [lambda n=n: run(n) for n in range(1, N_PIPE)])


def solution(mesh):
    return jax.shard_map(
        per_device,
        mesh=mesh,
        in_specs=(
            P(None, "seq", None),
            P(None, "seq", None),
            P(),
            P(),
            P("pipe", None),
            P("pipe", None, "mp"),
            P("pipe", None, "mp"),
            P("pipe", None, "mp"),
            P("pipe", "mp", None),
            P(None, "seq", None),
        ),
        out_specs=(P("pipe", None, "seq", "mp"), P("pipe", None, None, "seq", "mp")),
        check_vma=False,
    )
```
